32 devices in a mesh: batch: 4 (over x, core), tiles: 8 (over z, y).
Axes of the slice: x: 2, y: 2, z: 4, core: 2. Of those that a mesh axis runs over, the one named last changes fastest.
Arguments:
- hidden: bfloat16 [4, 4096, 3072], P('batch', 'tiles'), may hold values from -6 to 6
- frozen_queries: bfloat16 [4, 4096, 1536], P('batch', 'tiles'), may hold values from -108 to 108
- frozen_keys: bfloat16 [4, 4096, 1536], P('batch', 'tiles'), may hold values from -6.09 to 6.09
- frozen_values: bfloat16 [4, 4096, 1536], P('batch', 'tiles'), may hold values from -6 to 6
- reward_output_gradient: bfloat16 [4, 4096, 1536], P('batch', 'tiles'), may hold values from -6 to 6
- truncation_step: int32 [4], P('batch'), may hold values from 0 to 49
- modulation: float32 [50, 2, 3072], replicated, may hold values from -3 to 3
- adapter_down_weight: bfloat16 [3, 3072, 32], replicated, may hold values from -0.109375 to 0.109375
- adapter_up_weight: bfloat16 [3, 32, 1536], replicated, may hold values from -1 to 1
- window: int32 [32, 27], P('tiles'), may hold values from 0 to 1, as said below
Outputs:
- attended: bfloat16 [4, 4096, 1536], P('batch', 'tiles')
- grad_down: float32 [3, 3072, 32], replicated
- grad_up: float32 [3, 32, 1536], replicated
The draws below stay inside these ranges and needn't reach their ends.
Inputs may be any that keep to these rules, and one draw needn't show every extreme that they name: `window`: entry 13, the tile itself, is 1 for every tile.
All inputs are finite; a program needn't handle non-finite values.
Results may differ from the reference program's by a relative error of at most 0.012.
The reference program's roundings to bfloat16 on the way count: a program that leaves them out, or rounds other values in their place, can miss the bound.
Values may be sent and summed in bfloat16 or wider, within the bound.
A program may use at most 192 MiB of HBM per device.

```python
import math
import jax
import jax.numpy as jnp
from jax import lax

MODEL_WIDTH = 3072
HEADS = 12
HEAD = 128
ADAPTER_RANK = 32
TILE = 128
GF = 2
GR = 2
STEPS = 50
HEAD_FEATURES = 1536
SLAB = 512
TOKENS = 4096
TILES_ALL = 32
BATCH = 4
N_TILES = 8


def base_keys(key):
    return jnp.clip(jax.random.normal(jax.random.fold_in(key, 23), (BATCH, TOKENS, HEAD_FEATURES), jnp.float32), -6.0, 6.0)


def draw_hidden(key, part):
    values = jnp.clip(jax.random.normal(jax.random.fold_in(key, 11), (BATCH, TOKENS, MODEL_WIDTH), jnp.float32), -6.0, 6.0)
    return values.astype(jnp.bfloat16)


def draw_frozen_keys(key, part):
    values = base_keys(key)
    return values.astype(jnp.bfloat16)


def draw_frozen_queries(key, part):
    values = jnp.clip(jax.random.normal(jax.random.fold_in(key, 37), (BATCH, TOKENS, HEAD_FEATURES), jnp.float32), -6.0, 6.0)
    return values.astype(jnp.bfloat16)


def draw_window(key, part):
    slab_total = TILES_ALL // (GF * GR)
    levels = jax.random.randint(jax.random.fold_in(key, 5), (slab_total,), 2, 11)
    tile_level = jnp.repeat(levels, GF * GR)
    picks = jax.random.randint(jax.random.fold_in(key, 6), (TILES_ALL, 27), 0, 10)
    chosen = (picks < tile_level[:, None]).astype(jnp.int32)
    centre = (jnp.arange(27) == 13)[None, :]
    return jnp.where(centre, 1, chosen).astype(jnp.int32)


def with_ends(drawn, rng, least, high):
    longest = drawn.shape.index(max(drawn.shape))
    spots = []
    for shift in (0, 1):
        where = [jax.random.randint(jax.random.fold_in(rng, axis), (), 0, length) for axis, length in enumerate(drawn.shape)]
        where[longest] = (where[longest] + shift) % drawn.shape[longest]
        spots.append(tuple(where))
    return drawn.at[spots[0]].set(least).at[spots[1]].set(high)


def block_levels(stream_key, dims, split, least, top_value):
    loudness, own = 1.0, jax.random.fold_in(stream_key, 6)
    for dim, blocks in split:
        draws = jnp.exp(jax.random.uniform(jax.random.fold_in(own, dim), (blocks,), jnp.float32, least / len(split), top_value / len(split)))
        loudness = loudness * jnp.repeat(draws, dims[dim] // blocks).reshape([-1 if axis == dim else 1 for axis in range(len(dims))])
    return loudness


def scatter_about(rng, extent, width, most, cuts=(), held_as=jnp.bfloat16):
    array = jax.random.normal(rng, extent, jnp.float32) * width
    if len(cuts) > 0:
        array = block_levels(rng, extent, cuts, -0.22, 0.18) * array
    return jnp.clip(array, min=-most, max=most).astype(held_as)


def setup_inputs(seed: int = 0) -> dict:
    key_of = jax.random.split(jax.random.key(seed), 11)
    return {
        "hidden": draw_hidden(jax.random.fold_in(key_of[10], 71), 0),
        "frozen_queries": draw_frozen_queries(jax.random.fold_in(key_of[10], 71), 0),
        "frozen_keys": draw_frozen_keys(jax.random.fold_in(key_of[10], 71), 0),
        "frozen_values": scatter_about(key_of[3], (BATCH, TOKENS, HEAD_FEATURES), 1.0, 6.0, ((0, 4), (1, 8))),
        "reward_output_gradient": scatter_about(key_of[4], (BATCH, TOKENS, HEAD_FEATURES), 1.0, 6.0, ((0, 4), (1, 8))),
        "truncation_step": with_ends(jax.random.randint(key_of[5], (BATCH,), 0, STEPS), jax.random.fold_in(key_of[5], 1), 0, STEPS - 1).astype(jnp.int32),
        "modulation": scatter_about(key_of[6], (STEPS, 2, MODEL_WIDTH), 0.5, 3.0, (), jnp.float32),
        "adapter_down_weight": scatter_about(key_of[7], (3, MODEL_WIDTH, ADAPTER_RANK), MODEL_WIDTH ** -0.5, 0.109375),
        "adapter_up_weight": scatter_about(key_of[8], (3, ADAPTER_RANK, HEAD_FEATURES), ADAPTER_RANK ** -0.5, 1.0),
        "window": draw_window(jax.random.fold_in(key_of[10], 71), 0),
    }


precise_variant = lax.Precision.HIGHEST

def allowed_keys(window_rows, slab_index, slab_count):
    per_slab = GF * GR
    query_tile = jnp.arange(per_slab, dtype=jnp.int32)
    key_tile = jnp.arange(3 * per_slab, dtype=jnp.int32)
    key_side = key_tile // per_slab
    key_local = key_tile % per_slab
    frame_step = key_local[None, :] // GR - query_tile[:, None] // GR
    row_step = key_local[None, :] % GR - query_tile[:, None] % GR
    offset_code = (key_side[None, :] * 3 + frame_step + 1) * 3 + row_step + 1
    nearby = (jnp.abs(frame_step) <= 1) & (jnp.abs(row_step) <= 1)
    neighbour = slab_index + key_side - 1
    inside = (neighbour >= 0) & (neighbour < slab_count)
    offsets = jnp.arange(27, dtype=jnp.int32)
    listed = lax.optimization_barrier(jnp.sum(jnp.where(offset_code[:, :, None] == offsets[None, None, :], window_rows[:, None, :], 0), axis=2))
    tile_mask = nearby & inside[None, :] & (listed > 0)
    return jnp.repeat(jnp.repeat(tile_mask, TILE, axis=0), TILE, axis=1)

def modulate(hidden_rows, shift_scale):
    x_full = hidden_rows.astype(jnp.float32)
    row_mean = lax.optimization_barrier(jnp.mean(x_full, axis=1, keepdims=True))
    centred = x_full - row_mean
    variance = lax.optimization_barrier(jnp.mean(centred * centred, axis=1, keepdims=True))
    normed = centred * lax.rsqrt(variance + 1e-06)
    return normed * (1.0 + shift_scale[1][None, :]) + shift_scale[0][None, :]

def attend(queries, key_rows, value_rows, out_grad, allowed):
    scale_root = 1.0 / math.sqrt(HEAD)
    query_heads = queries.reshape(queries.shape[0], HEADS, HEAD).astype(jnp.float32)
    key_heads = key_rows.reshape(key_rows.shape[0], HEADS, HEAD).astype(jnp.float32)
    value_heads = value_rows.reshape(value_rows.shape[0], HEADS, HEAD).astype(jnp.float32)
    grad_heads = out_grad.reshape(out_grad.shape[0], HEADS, HEAD).astype(jnp.float32)
    scores = jnp.einsum('qhe,khe->hqk', query_heads, key_heads, precision=precise_variant) * scale_root
    scores = jnp.where(allowed[None], scores, -1e+30)
    row_max = lax.optimization_barrier(jnp.max(scores, axis=2, keepdims=True))
    weights = jnp.where(allowed[None], jnp.exp(scores - row_max), 0.0)
    totals = lax.optimization_barrier(jnp.sum(weights, axis=2, keepdims=True))
    probs = weights / totals
    probs_low = probs.astype(jnp.bfloat16).astype(jnp.float32)
    attended = jnp.einsum('hqk,khe->qhe', probs_low, value_heads, precision=precise_variant)
    prob_grad = jnp.einsum('qhe,khe->hqk', grad_heads, value_heads, precision=precise_variant)
    centre = lax.optimization_barrier(jnp.sum(probs * prob_grad, axis=2, keepdims=True))
    score_grad = (probs * (prob_grad - centre) * scale_root).astype(jnp.bfloat16).astype(jnp.float32)
    query_grad = jnp.einsum('hqk,khe->qhe', score_grad, key_heads, precision=precise_variant)
    key_grad = jnp.einsum('hqk,qhe->khe', score_grad, query_heads, precision=precise_variant)
    value_grad = jnp.einsum('hqk,qhe->khe', probs_low, grad_heads, precision=precise_variant)
    slab_rows = queries.shape[0]
    return (attended.reshape(slab_rows, HEAD_FEATURES), query_grad.reshape(slab_rows, HEAD_FEATURES), key_grad.reshape(3 * slab_rows, HEAD_FEATURES), value_grad.reshape(3 * slab_rows, HEAD_FEATURES))

def reference(hidden, frozen_queries, frozen_keys, frozen_values, reward_output_gradient, truncation_step, modulation, adapter_down_weight, adapter_up_weight, window):
    per_slab = GF * GR
    expanded_up_weight = adapter_up_weight.astype(jnp.float32)
    down_total = jnp.zeros((3, MODEL_WIDTH, ADAPTER_RANK), jnp.float32)
    up_total = jnp.zeros((3, ADAPTER_RANK, HEAD_FEATURES), jnp.float32)
    outputs = []
    for sample in range(BATCH):
        input_modulated = modulate(hidden[sample], modulation[truncation_step[sample]])
        input_reduced = lax.optimization_barrier(input_modulated.astype(jnp.bfloat16)).astype(jnp.float32)
        reduced_rank_input = jnp.einsum('mx,pxo->pmo', input_reduced, adapter_down_weight.astype(jnp.float32), precision=precise_variant).astype(jnp.bfloat16)
        projected_output = jnp.einsum('bfe,beg->bfg', reduced_rank_input.astype(jnp.float32), expanded_up_weight, precision=precise_variant)
        queries = (frozen_queries[sample] + projected_output[0]).astype(jnp.bfloat16)
        key_rows = (frozen_keys[sample] + projected_output[1]).astype(jnp.bfloat16)
        value_rows = (frozen_values[sample] + projected_output[2]).astype(jnp.bfloat16)
        zero_rows = jnp.zeros((SLAB, HEAD_FEATURES), jnp.bfloat16)
        key_padded = jnp.concatenate([zero_rows, key_rows, zero_rows], axis=0)
        value_padded = jnp.concatenate([zero_rows, value_rows, zero_rows], axis=0)
        out_grad = reward_output_gradient[sample]

        def visit(carry, slab_index):
            key_acc, value_acc = carry
            start = slab_index * SLAB
            query_slab = lax.dynamic_slice_in_dim(queries, start, SLAB, 0)
            key_slab = lax.dynamic_slice_in_dim(key_padded, start, 3 * SLAB, 0)
            value_slab = lax.dynamic_slice_in_dim(value_padded, start, 3 * SLAB, 0)
            grad_slab = lax.dynamic_slice_in_dim(out_grad, start, SLAB, 0)
            window_rows = lax.dynamic_slice_in_dim(window, slab_index * per_slab, per_slab, 0)
            allowed = allowed_keys(window_rows, slab_index, N_TILES)
            attended, query_grad, key_grad, value_grad = attend(query_slab, key_slab, value_slab, grad_slab, allowed)
            key_acc = lax.dynamic_update_slice_in_dim(key_acc, lax.dynamic_slice_in_dim(key_acc, start, 3 * SLAB, 0) + key_grad, start, 0)
            value_acc = lax.dynamic_update_slice_in_dim(value_acc, lax.dynamic_slice_in_dim(value_acc, start, 3 * SLAB, 0) + value_grad, start, 0)
            return ((key_acc, value_acc), (attended.astype(jnp.bfloat16), query_grad))
        zero_acc = jnp.zeros((TOKENS + 2 * SLAB, HEAD_FEATURES), jnp.float32)
        (key_acc, value_acc), (attended_all, query_all) = lax.scan(visit, (zero_acc, zero_acc), jnp.arange(N_TILES, dtype=jnp.int32))
        outputs.append(attended_all.reshape(TOKENS, HEAD_FEATURES))
        grads = jnp.stack([query_all.reshape(TOKENS, HEAD_FEATURES), key_acc[SLAB:SLAB + TOKENS], value_acc[SLAB:SLAB + TOKENS]])
        rank_grads = jnp.einsum('jth,jrh->jtr', grads, expanded_up_weight, precision=precise_variant)
        down_total = down_total + jnp.einsum('td,jtr->jdr', input_modulated, rank_grads, precision=precise_variant)
        up_total = up_total + jnp.einsum('jtr,jth->jrh', reduced_rank_input.astype(jnp.float32), grads, precision=precise_variant)
    norm_factor = 1.0 / math.sqrt(BATCH * TOKENS)
    return (jnp.stack(outputs), down_total * norm_factor, up_total * norm_factor)
```

```python
import functools
import math

import jax
import jax.numpy as jnp
from jax import lax
from jax.experimental import pallas as pl
from jax.experimental.pallas import tpu as pltpu
from jax.sharding import PartitionSpec as P

HEAD = 128
TILE = 128
GF = 2
GR = 2
LANES = 128
GROUPS = 3


def dot_nt(a, b):
    return lax.dot_general(
        a, b, (((1,), (1,)), ((), ())), preferred_element_type=jnp.float32
    )


def dot_tn(a, b):
    return lax.dot_general(
        a, b, (((0,), (0,)), ((), ())), preferred_element_type=jnp.float32
    )


def dot_nn(a, b):
    return jnp.dot(a, b, preferred_element_type=jnp.float32)


def project_kernel(groups, step_ref, hidden_ref, mod_ref, down_ref, up_ref, fq_ref, fk_ref, fv_ref,
                   x_ref, low_ref, q_ref, *kv_refs):
    x = hidden_ref[0].astype(jnp.float32)
    width = x.shape[1]
    mean = jnp.sum(x, axis=1, keepdims=True) * (1.0 / width)
    centred = x - mean
    variance = jnp.sum(centred * centred, axis=1, keepdims=True) * (1.0 / width)
    normed = centred * lax.rsqrt(variance + 1e-06)
    modulated = normed * (1.0 + mod_ref[0, 1:2, :]) + mod_ref[0, 0:1, :]
    x_low = modulated.astype(jnp.bfloat16)
    x_ref[...] = x_low
    low = dot_nn(x_low, down_ref[...]).astype(jnp.bfloat16)
    low_ref[...] = low
    q_ref[...] = (fq_ref[0].astype(jnp.float32) + dot_nn(low, up_ref[0])).astype(jnp.bfloat16)
    keys = (fk_ref[0].astype(jnp.float32) + dot_nn(low, up_ref[1])).astype(jnp.bfloat16)
    values = (fv_ref[0].astype(jnp.float32) + dot_nn(low, up_ref[2])).astype(jnp.bfloat16)
    part = keys.shape[1] // groups
    for g in range(groups):
        kv_refs[g][:, 0:part] = keys[:, g * part:(g + 1) * part]
        kv_refs[g][:, part:2 * part] = values[:, g * part:(g + 1) * part]
    kv_refs[0][:, 2 * part:2 * part + LANES] = low


def project(groups, step, hidden, modulation, down_cat, up_pad, fq, fk, fv):
    _, rows, width = hidden.shape
    across = fq.shape[2]
    block = TILE
    part = across // groups
    row3 = lambda i, s: (0, i, 0)
    row2 = lambda i, s: (i, 0)
    kv_widths = [2 * part + (LANES if g == 0 else 0) for g in range(groups)]
    return pl.pallas_call(
        functools.partial(project_kernel, groups),
        out_shape=[
            jax.ShapeDtypeStruct((rows, width), jnp.bfloat16),
            jax.ShapeDtypeStruct((rows, LANES), jnp.bfloat16),
            jax.ShapeDtypeStruct((rows, across), jnp.bfloat16),
        ] + [jax.ShapeDtypeStruct((rows, w), jnp.bfloat16) for w in kv_widths],
        grid_spec=pltpu.PrefetchScalarGridSpec(
            num_scalar_prefetch=1,
            grid=(rows // block,),
            in_specs=[
                pl.BlockSpec((1, block, width), row3),
                pl.BlockSpec((1, 2, width), lambda i, s: (s[0], 0, 0)),
                pl.BlockSpec(down_cat.shape, lambda i, s: (0, 0)),
                pl.BlockSpec(up_pad.shape, lambda i, s: (0, 0, 0)),
                pl.BlockSpec((1, block, across), row3),
                pl.BlockSpec((1, block, across), row3),
                pl.BlockSpec((1, block, across), row3),
            ],
            out_specs=[
                pl.BlockSpec((block, width), row2),
                pl.BlockSpec((block, LANES), row2),
                pl.BlockSpec((block, across), row2),
            ] + [pl.BlockSpec((block, w), row2) for w in kv_widths],
        ),
        name="project",
    )(step, hidden, modulation, down_cat, up_pad, fq, fk, fv)


def attend_kernel(rank, bias_ref, q_ref, g_ref, ko_ref, vo_ref, ks_ref, vs_ref, kr_ref, vr_ref,
                  lo_ref, ls_ref, lr_ref, up_ref, *rest):
    att_ref, rq_ref, rkv_ref, gup_ref, kl, vl, probs_s, grad_s = rest[-8:]
    rows = q_ref.shape[0]
    scale_root = 1.0 / math.sqrt(HEAD)
    scale_two = scale_root * math.log2(math.e)

    @pl.when(pl.program_id(0) == 0)
    def _():
        rq_ref[...] = jnp.zeros_like(rq_ref)
        rkv_ref[...] = jnp.zeros_like(rkv_ref)
        for s, low in enumerate((lo_ref, ls_ref, lr_ref)):
            kl[s * rows:(s + 1) * rows, HEAD:] = low[...]
            vl[s * rows:(s + 1) * rows, HEAD:] = low[...]

    for s, (k, v) in enumerate(((ko_ref, vo_ref), (ks_ref, vs_ref), (kr_ref, vr_ref))):
        kl[s * rows:(s + 1) * rows, 0:HEAD] = k[...]
        vl[s * rows:(s + 1) * rows, 0:HEAD] = v[...]

    for t in range(rows // TILE):
        span = slice(t * TILE, (t + 1) * TILE)
        scores = dot_nt(q_ref[span, :], kl[:, 0:HEAD]) * scale_two + bias_ref[t:t + 1, :]
        top = jnp.max(scores, axis=1, keepdims=True)
        weights = jnp.exp2(scores - top)
        inverse = 1.0 / jnp.sum(weights, axis=1, keepdims=True)
        probs = weights * inverse
        prob_grad = dot_nt(g_ref[0, span, :], vl[:, 0:HEAD])
        centre = jnp.sum(probs * prob_grad, axis=1, keepdims=True)
        probs_s[span, :] = probs.astype(jnp.bfloat16)
        grad_s[span, :] = (probs * (prob_grad - centre) * scale_root).astype(jnp.bfloat16)

    q_all = q_ref[...]
    g_all = g_ref[0]
    q_up = dot_nt(up_ref[1], q_all).astype(jnp.bfloat16)
    g_up = dot_nt(up_ref[2], g_all).astype(jnp.bfloat16)
    rkv_ref[0:rank, :] += dot_nn(q_up, grad_s[...])
    rkv_ref[rank:2 * rank, :] += dot_nn(g_up, probs_s[...])
    att = dot_nn(probs_s[...], vl[...])
    att_ref[0] = att[:, 0:HEAD].astype(jnp.bfloat16)
    low_v = att[:, HEAD:].astype(jnp.bfloat16)
    dq = dot_nn(grad_s[...], kl[...])
    dq_low = dq[:, 0:HEAD].astype(jnp.bfloat16)
    low_k = dq[:, HEAD:].astype(jnp.bfloat16)
    rq_ref[...] += dot_nt(up_ref[0], dq_low)
    gup_ref[0:rank, :] = dot_tn(lo_ref[...], dq_low)[0:rank, :]
    gup_ref[rank:2 * rank, :] = dot_tn(low_k, q_all)[rank:2 * rank, :]
    gup_ref[2 * rank:3 * rank, :] = dot_tn(low_v, g_all)[2 * rank:3 * rank, :]


def attend(group, groups, bias, q, g, kv, low_own, low_swap, low_relay, up, attended):
    rows, across = q.shape
    heads = across // HEAD // groups
    first = group * heads
    rank = up.shape[1]
    own, swap, relay = kv
    fixed = lambda h: (0, 0)
    key_spec = pl.BlockSpec((rows, HEAD), lambda h: (0, h))
    value_spec = pl.BlockSpec((rows, HEAD), lambda h: (0, heads + h))
    low_spec = pl.BlockSpec((rows, LANES), fixed)
    low_tail = pl.BlockSpec((rows, LANES), lambda h: (0, 2 * heads))
    in_specs = [
        pl.BlockSpec(bias.shape, fixed),
        pl.BlockSpec((rows, HEAD), lambda h: (0, first + h)),
        pl.BlockSpec((1, rows, HEAD), lambda h: (0, 0, first + h)),
        key_spec, value_spec, key_spec, value_spec, key_spec, value_spec,
        low_spec, low_tail, low_tail,
        pl.BlockSpec((3, rank, HEAD), lambda h: (0, 0, first + h)),
    ]
    args = [bias, q, g, own, own, swap, swap, relay, relay, low_own, low_swap, low_relay, up]
    aliases = {}
    if attended is not None:
        in_specs.append(pl.BlockSpec(memory_space=pl.ANY))
        aliases = {len(args): 0}
        args.append(attended)
    flops = heads * 2 * rows * 3 * rows * HEAD * 8
    return pl.pallas_call(
        functools.partial(attend_kernel, rank),
        grid=(heads,),
        out_shape=[
            jax.ShapeDtypeStruct((1, rows, across), jnp.bfloat16),
            jax.ShapeDtypeStruct((rank, rows), jnp.float32),
            jax.ShapeDtypeStruct((2 * rank, 3 * rows), jnp.float32),
            jax.ShapeDtypeStruct((3 * rank, heads * HEAD), jnp.float32),
        ],
        in_specs=in_specs,
        out_specs=[
            pl.BlockSpec((1, rows, HEAD), lambda h: (0, 0, first + h)),
            pl.BlockSpec((rank, rows), fixed),
            pl.BlockSpec((2 * rank, 3 * rows), fixed),
            pl.BlockSpec((3 * rank, HEAD), lambda h: (0, h)),
        ],
        scratch_shapes=[
            pltpu.VMEM((3 * rows, 2 * HEAD), jnp.bfloat16),
            pltpu.VMEM((3 * rows, 2 * HEAD), jnp.bfloat16),
            pltpu.VMEM((rows, 3 * rows), jnp.bfloat16),
            pltpu.VMEM((rows, 3 * rows), jnp.bfloat16),
        ],
        input_output_aliases=aliases,
        cost_estimate=pl.CostEstimate(
            flops=flops, bytes_accessed=heads * rows * HEAD * 20,
            transcendentals=heads * rows * 3 * rows,
        ),
        name="attend",
    )(*args)


def mask_bias(window_rows, sides, present):
    per_slab = GF * GR
    query_tile = jnp.arange(per_slab, dtype=jnp.int32)
    key_local = jnp.tile(query_tile, 3)
    key_side = jnp.repeat(jnp.stack(sides), per_slab)
    here = jnp.repeat(jnp.stack(present), per_slab)
    frame_step = key_local[None, :] // GR - query_tile[:, None] // GR
    row_step = key_local[None, :] % GR - query_tile[:, None] % GR
    code = (key_side[None, :] * 3 + frame_step + 1) * 3 + row_step + 1
    nearby = (jnp.abs(frame_step) <= 1) & (jnp.abs(row_step) <= 1)
    offsets = jnp.arange(27, dtype=jnp.int32)
    listed = jnp.sum(
        jnp.where(code[:, :, None] == offsets[None, None, :], window_rows[:, None, :], 0), axis=2
    )
    allowed = nearby & here[None, :] & (listed > 0)
    return jnp.repeat(jnp.where(allowed, 0.0, -1e30).astype(jnp.float32), TILE, axis=1)


def per_device(
    hidden,
    frozen_queries,
    frozen_keys,
    frozen_values,
    reward_output_gradient,
    truncation_step,
    modulation,
    adapter_down_weight,
    adapter_up_weight,
    window,
):
    slab_rows, width = hidden.shape[1:]
    across = frozen_queries.shape[2]
    rank = adapter_up_weight.shape[1]
    count = lax.axis_size("tiles")
    index = lax.axis_index("tiles")
    even = index % 2 == 0
    heads = across // HEAD
    groups = GROUPS if heads % GROUPS == 0 else 1

    down_cat = jnp.concatenate(
        [adapter_down_weight[j] for j in range(3)]
        + [jnp.zeros((width, LANES - 3 * rank), jnp.bfloat16)], axis=1
    )
    up_pad = jnp.stack([
        jnp.pad(adapter_up_weight[j], ((j * rank, LANES - (j + 1) * rank), (0, 0)))
        for j in range(3)
    ])
    x_low, low, queries, *kv = project(
        groups, truncation_step, hidden, modulation, down_cat, up_pad,
        frozen_queries, frozen_keys, frozen_values,
    )

    swap_pairs = [(i, i ^ 1) for i in range(count)]
    relay_pairs = [(i, i + 2) for i in range(0, count - 2, 2)]
    relay_pairs += [(i, i - 2) for i in range(3, count, 2)]
    return_pairs = [(i, i - 1) for i in range(2, count, 2)]
    return_pairs += [(i, i + 1) for i in range(1, count - 1, 2)]

    zero, one, two = (jnp.int32(i) for i in range(3))
    swap_side = jnp.where(even, two, zero)
    relay_side = jnp.where(even, zero, two)
    relay_here = jnp.where(even, index >= 1, index < count - 1)
    bias = mask_bias(
        window, (one, swap_side, relay_side), (jnp.bool_(True), jnp.bool_(True), relay_here)
    )

    swapped = [lax.ppermute(part, "tiles", swap_pairs) for part in kv]
    relayed = [lax.ppermute(part, "tiles", relay_pairs) for part in swapped]

    attended = None
    rq_total, rkv_total, ups = 0.0, 0.0, []
    for g in range(groups):
        attended, rq, rkv, gup = attend(
            g, groups, bias, queries, reward_output_gradient,
            (kv[g], swapped[g], relayed[g]), low, swapped[0], relayed[0],
            adapter_up_weight, attended,
        )
        rq_total, rkv_total = rq_total + rq, rkv_total + rkv
        ups.append(gup)

    from_swap = lax.ppermute(rkv_total[:, slab_rows:2 * slab_rows], "tiles", swap_pairs)
    from_relay = lax.ppermute(rkv_total[:, 2 * slab_rows:], "tiles", return_pairs)
    owned = rkv_total[:, 0:slab_rows] + from_swap + from_relay
    rank_grads = jnp.concatenate([rq_total, owned], axis=0).astype(jnp.bfloat16)
    down_terms = jnp.dot(rank_grads, x_low, preferred_element_type=jnp.float32)
    norm_factor = 1.0 / math.sqrt(
        hidden.shape[0] * lax.axis_size("batch") * slab_rows * count
    )
    terms = jnp.concatenate([down_terms] + ups, axis=1) * norm_factor
    total = lax.psum(terms, ("batch", "tiles"))
    grad_down = total[:, 0:width].reshape(3, rank, width).transpose(0, 2, 1)
    grad_up = total[:, width:].reshape(3, rank, across)
    return (attended, grad_down, grad_up)


def solution(mesh):
    placed = (
        P("batch", "tiles", None),
        P("batch", "tiles", None),
        P("batch", "tiles", None),
        P("batch", "tiles", None),
        P("batch", "tiles", None),
        P("batch"),
        P(),
        P(),
        P(),
        P("tiles", None),
    )
    return jax.shard_map(
        per_device,
        mesh=mesh,
        in_specs=placed,
        out_specs=(P("batch", "tiles", None), P(), P()),
        check_vma=False,
    )
```

```python
import functools
import math

import jax
import jax.numpy as jnp
from jax import lax
from jax.experimental import pallas as pl
from jax.experimental.pallas import tpu as pltpu
from jax.sharding import PartitionSpec as P

HEAD = 128
TILE = 128
GF = 2
GR = 2
LANES = 128
GROUPS = 3


def dot_nt(a, b):
    return lax.dot_general(
        a, b, (((1,), (1,)), ((), ())), preferred_element_type=jnp.float32
    )


def dot_tn(a, b):
    return lax.dot_general(
        a, b, (((0,), (0,)), ((), ())), preferred_element_type=jnp.float32
    )


def dot_nn(a, b):
    return jnp.dot(a, b, preferred_element_type=jnp.float32)


def project_kernel(groups, step_ref, hidden_ref, mod_ref, down_ref, up_ref, fq_ref, fk_ref, fv_ref,
                   x_ref, low_ref, q_ref, *kv_refs):
    x = hidden_ref[0].astype(jnp.float32)
    width = x.shape[1]
    mean = jnp.sum(x, axis=1, keepdims=True) * (1.0 / width)
    centred = x - mean
    variance = jnp.sum(centred * centred, axis=1, keepdims=True) * (1.0 / width)
    normed = centred * lax.rsqrt(variance + 1e-06)
    modulated = normed * (1.0 + mod_ref[0, 1:2, :]) + mod_ref[0, 0:1, :]
    x_low = modulated.astype(jnp.bfloat16)
    x_ref[...] = x_low
    low = dot_nn(x_low, down_ref[...]).astype(jnp.bfloat16)
    low_ref[...] = low
    q_ref[...] = (fq_ref[0].astype(jnp.float32) + dot_nn(low, up_ref[0])).astype(jnp.bfloat16)
    keys = (fk_ref[0].astype(jnp.float32) + dot_nn(low, up_ref[1])).astype(jnp.bfloat16)
    values = (fv_ref[0].astype(jnp.float32) + dot_nn(low, up_ref[2])).astype(jnp.bfloat16)
    part = keys.shape[1] // groups
    for g in range(groups):
        kv_refs[g][:, 0:part] = keys[:, g * part:(g + 1) * part]
        kv_refs[g][:, part:2 * part] = values[:, g * part:(g + 1) * part]
    kv_refs[0][:, 2 * part:2 * part + LANES] = low


def project(groups, step, hidden, modulation, down_cat, up_pad, fq, fk, fv):
    _, rows, width = hidden.shape
    across = fq.shape[2]
    block = TILE
    part = across // groups
    row3 = lambda i, s: (0, i, 0)
    row2 = lambda i, s: (i, 0)
    kv_widths = [2 * part + (LANES if g == 0 else 0) for g in range(groups)]
    return pl.pallas_call(
        functools.partial(project_kernel, groups),
        out_shape=[
            jax.ShapeDtypeStruct((rows, width), jnp.bfloat16),
            jax.ShapeDtypeStruct((rows, LANES), jnp.bfloat16),
            jax.ShapeDtypeStruct((rows, across), jnp.bfloat16),
        ] + [jax.ShapeDtypeStruct((rows, w), jnp.bfloat16) for w in kv_widths],
        grid_spec=pltpu.PrefetchScalarGridSpec(
            num_scalar_prefetch=1,
            grid=(rows // block,),
            in_specs=[
                pl.BlockSpec((1, block, width), row3),
                pl.BlockSpec((1, 2, width), lambda i, s: (s[0], 0, 0)),
                pl.BlockSpec(down_cat.shape, lambda i, s: (0, 0)),
                pl.BlockSpec(up_pad.shape, lambda i, s: (0, 0, 0)),
                pl.BlockSpec((1, block, across), row3),
                pl.BlockSpec((1, block, across), row3),
                pl.BlockSpec((1, block, across), row3),
            ],
            out_specs=[
                pl.BlockSpec((block, width), row2),
                pl.BlockSpec((block, LANES), row2),
                pl.BlockSpec((block, across), row2),
            ] + [pl.BlockSpec((block, w), row2) for w in kv_widths],
        ),
        name="project",
    )(step, hidden, modulation, down_cat, up_pad, fq, fk, fv)


def attend_kernel(rank, bias_ref, q_ref, g_ref, ko_ref, vo_ref, ks_ref, vs_ref, kr_ref, vr_ref,
                  lo_ref, ls_ref, lr_ref, up_ref, *rest):
    att_ref, rq_ref, rkv_ref, gup_ref, kl, vl, probs_s, grad_s = rest[-8:]
    rows = q_ref.shape[0]
    scale_root = 1.0 / math.sqrt(HEAD)
    scale_two = scale_root * math.log2(math.e)

    @pl.when(pl.program_id(0) == 0)
    def _():
        rq_ref[...] = jnp.zeros_like(rq_ref)
        rkv_ref[...] = jnp.zeros_like(rkv_ref)
        for s, low in enumerate((lo_ref, ls_ref, lr_ref)):
            kl[s * rows:(s + 1) * rows, HEAD:] = low[...]
            vl[s * rows:(s + 1) * rows, HEAD:] = low[...]

    for s, (k, v) in enumerate(((ko_ref, vo_ref), (ks_ref, vs_ref), (kr_ref, vr_ref))):
        kl[s * rows:(s + 1) * rows, 0:HEAD] = k[...]
        vl[s * rows:(s + 1) * rows, 0:HEAD] = v[...]

    for t in range(rows // TILE):
        span = slice(t * TILE, (t + 1) * TILE)
        scores = dot_nt(q_ref[span, :], kl[:, 0:HEAD]) * scale_two + bias_ref[t:t + 1, :]
        top = jnp.max(scores, axis=1, keepdims=True)
        weights = jnp.exp2(scores - top)
        inverse = 1.0 / jnp.sum(weights, axis=1, keepdims=True)
        probs = weights * inverse
        prob_grad = dot_nt(g_ref[0, span, :], vl[:, 0:HEAD])
        centre = jnp.sum(probs * prob_grad, axis=1, keepdims=True)
        probs_s[span, :] = probs.astype(jnp.bfloat16)
        grad_s[span, :] = (probs * (prob_grad - centre) * scale_root).astype(jnp.bfloat16)

    q_all = q_ref[...]
    g_all = g_ref[0]
    q_up = dot_nt(up_ref[1], q_all).astype(jnp.bfloat16)
    g_up = dot_nt(up_ref[2], g_all).astype(jnp.bfloat16)
    rkv_ref[0:rank, :] += dot_nn(q_up, grad_s[...])
    rkv_ref[rank:2 * rank, :] += dot_nn(g_up, probs_s[...])
    att = dot_nn(probs_s[...], vl[...])
    att_ref[0] = att[:, 0:HEAD].astype(jnp.bfloat16)
    low_v = att[:, HEAD:].astype(jnp.bfloat16)
    dq = dot_nn(grad_s[...], kl[...])
    dq_low = dq[:, 0:HEAD].astype(jnp.bfloat16)
    low_k = dq[:, HEAD:].astype(jnp.bfloat16)
    rq_ref[...] += dot_nt(up_ref[0], dq_low)
    gup_ref[0:rank, :] = dot_tn(lo_ref[...], dq_low)[0:rank, :]
    gup_ref[rank:2 * rank, :] = dot_tn(low_k, q_all)[rank:2 * rank, :]
    gup_ref[2 * rank:3 * rank, :] = dot_tn(low_v, g_all)[2 * rank:3 * rank, :]


def attend(group, groups, bias, q, g, kv, low_own, low_swap, low_relay, up, attended):
    rows, across = q.shape
    heads = across // HEAD // groups
    first = group * heads
    rank = up.shape[1]
    own, swap, relay = kv
    fixed = lambda h: (0, 0)
    key_spec = pl.BlockSpec((rows, HEAD), lambda h: (0, h))
    value_spec = pl.BlockSpec((rows, HEAD), lambda h: (0, heads + h))
    low_spec = pl.BlockSpec((rows, LANES), fixed)
    low_tail = pl.BlockSpec((rows, LANES), lambda h: (0, 2 * heads))
    in_specs = [
        pl.BlockSpec(bias.shape, fixed),
        pl.BlockSpec((rows, HEAD), lambda h: (0, first + h)),
        pl.BlockSpec((1, rows, HEAD), lambda h: (0, 0, first + h)),
        key_spec, value_spec, key_spec, value_spec, key_spec, value_spec,
        low_spec, low_tail, low_tail,
        pl.BlockSpec((3, rank, HEAD), lambda h: (0, 0, first + h)),
    ]
    args = [bias, q, g, own, own, swap, swap, relay, relay, low_own, low_swap, low_relay, up]
    aliases = {}
    if attended is not None:
        in_specs.append(pl.BlockSpec(memory_space=pl.ANY))
        aliases = {len(args): 0}
        args.append(attended)
    flops = heads * 2 * rows * 3 * rows * HEAD * 8
    return pl.pallas_call(
        functools.partial(attend_kernel, rank),
        grid=(heads,),
        out_shape=[
            jax.ShapeDtypeStruct((1, rows, across), jnp.bfloat16),
            jax.ShapeDtypeStruct((rank, rows), jnp.float32),
            jax.ShapeDtypeStruct((2 * rank, 3 * rows), jnp.float32),
            jax.ShapeDtypeStruct((3 * rank, heads * HEAD), jnp.float32),
        ],
        in_specs=in_specs,
        out_specs=[
            pl.BlockSpec((1, rows, HEAD), lambda h: (0, 0, first + h)),
            pl.BlockSpec((rank, rows), fixed),
            pl.BlockSpec((2 * rank, 3 * rows), fixed),
            pl.BlockSpec((3 * rank, HEAD), lambda h: (0, h)),
        ],
        scratch_shapes=[
            pltpu.VMEM((3 * rows, 2 * HEAD), jnp.bfloat16),
            pltpu.VMEM((3 * rows, 2 * HEAD), jnp.bfloat16),
            pltpu.VMEM((rows, 3 * rows), jnp.bfloat16),
            pltpu.VMEM((rows, 3 * rows), jnp.bfloat16),
        ],
        input_output_aliases=aliases,
        cost_estimate=pl.CostEstimate(
            flops=flops, bytes_accessed=heads * rows * HEAD * 20,
            transcendentals=heads * rows * 3 * rows,
        ),
        name="attend",
    )(*args)


def reduce_kernel(nb, nt, terms_ref, out_ref, first, partial, second, final,
                  send1, recv1, send2, recv2, send3, recv3, send4, recv4):
    mine_b = lax.axis_index("batch")
    mine_t = lax.axis_index("tiles")
    barrier = pltpu.get_barrier_semaphore()
    for d in range(1, nb):
        pl.semaphore_signal(barrier, inc=1, device_id={"batch": lax.rem(mine_b + d, nb)},
                            device_id_type=pl.DeviceIdType.MESH)
    for d in range(1, nt):
        pl.semaphore_signal(barrier, inc=1, device_id={"tiles": lax.rem(mine_t + d, nt)},
                            device_id_type=pl.DeviceIdType.MESH)
    pl.semaphore_wait(barrier, nb + nt - 2)

    def launch(source, target, send, recv, axis, peer):
        copy = pltpu.make_async_remote_copy(
            src_ref=source, dst_ref=target, send_sem=send, recv_sem=recv,
            device_id={axis: peer}, device_id_type=pl.DeviceIdType.MESH,
        )
        copy.start()
        return copy

    copies = []
    for d in range(1, nb):
        peer = lax.rem(mine_b + d, nb)
        copies.append(launch(terms_ref.at[peer], first.at[d - 1], send1.at[d - 1],
                             recv1.at[d - 1], "batch", peer))
    for copy in copies:
        copy.wait()
    total = terms_ref[mine_b].astype(jnp.float32)
    for d in range(nb - 1):
        total = total + first[d].astype(jnp.float32)
    partial[...] = total.astype(jnp.bfloat16)

    copies = []
    for d in range(1, nt):
        peer = lax.rem(mine_t + d, nt)
        copies.append(launch(partial.at[peer], second.at[d - 1], send2.at[d - 1],
                             recv2.at[d - 1], "tiles", peer))
    for copy in copies:
        copy.wait()
    total = partial[mine_t].astype(jnp.float32)
    for d in range(nt - 1):
        total = total + second[d].astype(jnp.float32)
    final[...] = total.astype(jnp.bfloat16)

    copies = []
    for d in range(1, nt):
        peer = lax.rem(mine_t + d, nt)
        copies.append(launch(final, out_ref.at[mine_b, mine_t], send3.at[d - 1],
                             recv3.at[d - 1], "tiles", peer))
    out_ref[mine_b, mine_t] = final[...]
    for copy in copies:
        copy.wait()

    copies = []
    for d in range(1, nb):
        peer = lax.rem(mine_b + d, nb)
        copies.append(launch(out_ref.at[mine_b], out_ref.at[mine_b], send4.at[d - 1],
                             recv4.at[d - 1], "batch", peer))
    for copy in copies:
        copy.wait()


def reduce_all(terms):
    nb, nt, rows, lanes = terms.shape
    dma = pltpu.SemaphoreType.DMA
    return pl.pallas_call(
        functools.partial(reduce_kernel, nb, nt),
        out_shape=jax.ShapeDtypeStruct(terms.shape, jnp.bfloat16),
        in_specs=[pl.BlockSpec(memory_space=pltpu.VMEM)],
        out_specs=pl.BlockSpec(memory_space=pltpu.VMEM),
        scratch_shapes=[
            pltpu.VMEM((nb - 1, nt, rows, lanes), jnp.bfloat16),
            pltpu.VMEM((nt, rows, lanes), jnp.bfloat16),
            pltpu.VMEM((nt - 1, rows, lanes), jnp.bfloat16),
            pltpu.VMEM((rows, lanes), jnp.bfloat16),
            dma((nb - 1,)), dma((nb - 1,)), dma((nt - 1,)), dma((nt - 1,)),
            dma((nt - 1,)), dma((nt - 1,)), dma((nb - 1,)), dma((nb - 1,)),
        ],
        compiler_params=pltpu.CompilerParams(collective_id=0, has_side_effects=True),
        name="reduce_all",
    )(terms)


def summed_everywhere(terms):
    nb, nt = lax.axis_size("batch"), lax.axis_size("tiles")
    rows, columns = terms.shape
    pieces = (rows // 16) * (columns // LANES)
    share = -(-pieces // (nb * nt))
    tiled = terms.astype(jnp.bfloat16).reshape(rows // 16, 16, columns // LANES, LANES)
    tiled = tiled.transpose(0, 2, 1, 3).reshape(pieces, 16, LANES)
    tiled = jnp.pad(tiled, ((0, share * nb * nt - pieces), (0, 0), (0, 0)))
    total = reduce_all(tiled.reshape(nb, nt, share * 16, LANES))
    total = total.reshape(share * nb * nt, 16, LANES)[0:pieces]
    total = total.reshape(rows // 16, columns // LANES, 16, LANES).transpose(0, 2, 1, 3)
    return total.reshape(rows, columns).astype(jnp.float32)


def mask_bias(window_rows, sides, present):
    per_slab = GF * GR
    query_tile = jnp.arange(per_slab, dtype=jnp.int32)
    key_local = jnp.tile(query_tile, 3)
    key_side = jnp.repeat(jnp.stack(sides), per_slab)
    here = jnp.repeat(jnp.stack(present), per_slab)
    frame_step = key_local[None, :] // GR - query_tile[:, None] // GR
    row_step = key_local[None, :] % GR - query_tile[:, None] % GR
    code = (key_side[None, :] * 3 + frame_step + 1) * 3 + row_step + 1
    nearby = (jnp.abs(frame_step) <= 1) & (jnp.abs(row_step) <= 1)
    offsets = jnp.arange(27, dtype=jnp.int32)
    listed = jnp.sum(
        jnp.where(code[:, :, None] == offsets[None, None, :], window_rows[:, None, :], 0), axis=2
    )
    allowed = nearby & here[None, :] & (listed > 0)
    return jnp.repeat(jnp.where(allowed, 0.0, -1e30).astype(jnp.float32), TILE, axis=1)


def per_device(
    hidden,
    frozen_queries,
    frozen_keys,
    frozen_values,
    reward_output_gradient,
    truncation_step,
    modulation,
    adapter_down_weight,
    adapter_up_weight,
    window,
):
    slab_rows, width = hidden.shape[1:]
    across = frozen_queries.shape[2]
    rank = adapter_up_weight.shape[1]
    count = lax.axis_size("tiles")
    index = lax.axis_index("tiles")
    even = index % 2 == 0
    heads = across // HEAD
    groups = GROUPS if heads % GROUPS == 0 else 1

    down_cat = jnp.concatenate(
        [adapter_down_weight[j] for j in range(3)]
        + [jnp.zeros((width, LANES - 3 * rank), jnp.bfloat16)], axis=1
    )
    up_pad = jnp.stack([
        jnp.pad(adapter_up_weight[j], ((j * rank, LANES - (j + 1) * rank), (0, 0)))
        for j in range(3)
    ])
    x_low, low, queries, *kv = project(
        groups, truncation_step, hidden, modulation, down_cat, up_pad,
        frozen_queries, frozen_keys, frozen_values,
    )

    swap_pairs = [(i, i ^ 1) for i in range(count)]
    relay_pairs = [(i, i + 2) for i in range(0, count - 2, 2)]
    relay_pairs += [(i, i - 2) for i in range(3, count, 2)]
    return_pairs = [(i, i - 1) for i in range(2, count, 2)]
    return_pairs += [(i, i + 1) for i in range(1, count - 1, 2)]

    zero, one, two = (jnp.int32(i) for i in range(3))
    swap_side = jnp.where(even, two, zero)
    relay_side = jnp.where(even, zero, two)
    relay_here = jnp.where(even, index >= 1, index < count - 1)
    bias = mask_bias(
        window, (one, swap_side, relay_side), (jnp.bool_(True), jnp.bool_(True), relay_here)
    )

    swapped = [lax.ppermute(part, "tiles", swap_pairs) for part in kv]
    hops = lambda part: lax.ppermute(part, "tiles", relay_pairs)
    relayed = [hops(part) for part in swapped[0:2]]

    attended = None
    rq_total, rkv_total, ups = 0.0, 0.0, []
    for g in range(groups):
        attended, rq, rkv, gup = attend(
            g, groups, bias, queries, reward_output_gradient,
            (kv[g], swapped[g], relayed[g]), low, swapped[0], relayed[0],
            adapter_up_weight, attended,
        )
        if g + 2 < groups:
            waiting, attended = lax.optimization_barrier((swapped[g + 2], attended))
            relayed.append(hops(waiting))
        rq_total, rkv_total = rq_total + rq, rkv_total + rkv
        ups.append(gup)

    from_swap = lax.ppermute(rkv_total[:, slab_rows:2 * slab_rows], "tiles", swap_pairs)
    from_relay = lax.ppermute(rkv_total[:, 2 * slab_rows:], "tiles", return_pairs)
    owned = rkv_total[:, 0:slab_rows] + from_swap + from_relay
    rank_grads = jnp.concatenate([rq_total, owned], axis=0).astype(jnp.bfloat16)
    down_terms = jnp.dot(rank_grads, x_low, preferred_element_type=jnp.float32)
    norm_factor = 1.0 / math.sqrt(
        hidden.shape[0] * lax.axis_size("batch") * slab_rows * count
    )
    terms = jnp.concatenate([down_terms] + ups, axis=1) * norm_factor
    total = summed_everywhere(terms)
    grad_down = total[:, 0:width].reshape(3, rank, width).transpose(0, 2, 1)
    grad_up = total[:, width:].reshape(3, rank, across)
    return (attended, grad_down, grad_up)


def solution(mesh):
    placed = (
        P("batch", "tiles", None),
        P("batch", "tiles", None),
        P("batch", "tiles", None),
        P("batch", "tiles", None),
        P("batch", "tiles", None),
        P("batch"),
        P(),
        P(),
        P(),
        P("tiles", None),
    )
    return jax.shard_map(
        per_device,
        mesh=mesh,
        in_specs=placed,
        out_specs=(P("batch", "tiles", None), P(), P()),
        check_vma=False,
    )
```

```python
import functools
import math

import jax
import jax.numpy as jnp
from jax import lax
from jax.experimental import pallas as pl
from jax.experimental.pallas import tpu as pltpu
from jax.sharding import PartitionSpec as P

HEAD = 128
TILE = 128
GF = 2
GR = 2
LANES = 128


def dot_nt(a, b):
    return lax.dot_general(
        a, b, (((1,), (1,)), ((), ())), preferred_element_type=jnp.float32
    )


def dot_tn(a, b):
    return lax.dot_general(
        a, b, (((0,), (0,)), ((), ())), preferred_element_type=jnp.float32
    )


def dot_nn(a, b):
    return jnp.dot(a, b, preferred_element_type=jnp.float32)


def project_kernel(step_ref, hidden_ref, mod_ref, down_ref, up_ref, fq_ref, fk_ref, fv_ref,
                   x_ref, low_ref, q_ref, kv_ref):
    x = hidden_ref[0].astype(jnp.float32)
    width = x.shape[1]
    mean = jnp.sum(x, axis=1, keepdims=True) * (1.0 / width)
    centred = x - mean
    variance = jnp.sum(centred * centred, axis=1, keepdims=True) * (1.0 / width)
    normed = centred * lax.rsqrt(variance + 1e-06)
    modulated = normed * (1.0 + mod_ref[0, 1:2, :]) + mod_ref[0, 0:1, :]
    x_low = modulated.astype(jnp.bfloat16)
    x_ref[...] = x_low
    low = dot_nn(x_low, down_ref[...]).astype(jnp.bfloat16)
    low_ref[...] = low
    q_ref[...] = (fq_ref[0].astype(jnp.float32) + dot_nn(low, up_ref[0])).astype(jnp.bfloat16)
    keys = (fk_ref[0].astype(jnp.float32) + dot_nn(low, up_ref[1])).astype(jnp.bfloat16)
    values = (fv_ref[0].astype(jnp.float32) + dot_nn(low, up_ref[2])).astype(jnp.bfloat16)
    for h in range(keys.shape[1] // HEAD):
        kv_ref[h, :, 0:HEAD] = keys[:, h * HEAD:(h + 1) * HEAD]
        kv_ref[h, :, HEAD:] = values[:, h * HEAD:(h + 1) * HEAD]


def project(step, hidden, modulation, down_cat, up_pad, fq, fk, fv):
    _, rows, width = hidden.shape
    across = fq.shape[2]
    block = TILE
    heads = across // HEAD
    row3 = lambda i, s: (0, i, 0)
    row2 = lambda i, s: (i, 0)
    return pl.pallas_call(
        project_kernel,
        out_shape=[
            jax.ShapeDtypeStruct((rows, width), jnp.bfloat16),
            jax.ShapeDtypeStruct((rows, LANES), jnp.bfloat16),
            jax.ShapeDtypeStruct((rows, across), jnp.bfloat16),
            jax.ShapeDtypeStruct((heads, rows, 2 * HEAD), jnp.bfloat16),
        ],
        grid_spec=pltpu.PrefetchScalarGridSpec(
            num_scalar_prefetch=1,
            grid=(rows // block,),
            in_specs=[
                pl.BlockSpec((1, block, width), row3),
                pl.BlockSpec((1, 2, width), lambda i, s: (s[0], 0, 0)),
                pl.BlockSpec(down_cat.shape, lambda i, s: (0, 0)),
                pl.BlockSpec(up_pad.shape, lambda i, s: (0, 0, 0)),
                pl.BlockSpec((1, block, across), row3),
                pl.BlockSpec((1, block, across), row3),
                pl.BlockSpec((1, block, across), row3),
            ],
            out_specs=[
                pl.BlockSpec((block, width), row2),
                pl.BlockSpec((block, LANES), row2),
                pl.BlockSpec((block, across), row2),
                pl.BlockSpec((heads, block, 2 * HEAD), lambda i, s: (0, i, 0)),
            ],
        ),
        name="project",
    )(step, hidden, modulation, down_cat, up_pad, fq, fk, fv)


def attend_kernel(rank, count, bias_ref, q_ref, g_ref, kv_ref, low_ref, up_ref,
                  att_ref, rq_ref, own_ref, gup_ref,
                  kv_swap, kv_relay, low_swap, low_relay, kl, vl, probs_s, grad_s, rkv,
                  r_out, r_in, swap_send, swap_recv, relay_send, relay_recv,
                  low_send, low_recv, r_send, r_recv):
    heads, rows = kv_ref.shape[0], q_ref.shape[0]
    index = lax.axis_index("tiles")
    odd = lax.rem(index, 2)
    partner = index + 1 - 2 * odd
    target = lax.rem(index + 2 - 4 * odd + count, count)
    source = lax.rem(index - 2 + 4 * odd + count, count)
    other = lax.rem(index - 1 + 2 * odd + count, count)
    barrier = pltpu.get_barrier_semaphore()
    for peer in (partner, target, source, other):
        pl.semaphore_signal(barrier, inc=1, device_id={"tiles": peer},
                            device_id_type=pl.DeviceIdType.MESH)
    pl.semaphore_wait(barrier, 4)

    def remote(src, dst, send, recv, peer):
        return pltpu.make_async_remote_copy(
            src_ref=src, dst_ref=dst, send_sem=send, recv_sem=recv,
            device_id={"tiles": peer}, device_id_type=pl.DeviceIdType.MESH,
        )

    def swap(h):
        return remote(kv_ref.at[h], kv_swap.at[h], swap_send.at[h], swap_recv.at[h], partner)

    def relay(h):
        return remote(kv_swap.at[h], kv_relay.at[h], relay_send.at[h], relay_recv.at[h], target)

    def each(step):
        lax.fori_loop(0, heads, lambda h, c: (step(h), c)[1], 0)

    low_first = remote(low_ref, low_swap, low_send.at[0], low_recv.at[0], partner)
    low_next = remote(low_swap, low_relay, low_send.at[1], low_recv.at[1], target)
    low_first.start()
    each(lambda h: swap(h).start())
    rq_ref[...] = jnp.zeros_like(rq_ref)
    rkv[...] = jnp.zeros_like(rkv)
    low_first.wait_recv()
    low_next.start()
    swap(0).wait_recv()
    relay(0).start()
    low_next.wait_recv()
    for s, low in enumerate((low_ref, low_swap, low_relay)):
        kl[s * rows:(s + 1) * rows, HEAD:] = low[...]
        vl[s * rows:(s + 1) * rows, HEAD:] = low[...]
    scale_root = 1.0 / math.sqrt(HEAD)
    scale_two = scale_root * math.log2(math.e)

    def one_head(h, carry):
        @pl.when(h + 1 < heads)
        def _():
            swap(h + 1).wait_recv()
            relay(h + 1).start()

        relay(h).wait_recv()
        for s, part in enumerate((kv_ref, kv_swap, kv_relay)):
            kl[s * rows:(s + 1) * rows, 0:HEAD] = part[h, :, 0:HEAD]
            vl[s * rows:(s + 1) * rows, 0:HEAD] = part[h, :, HEAD:]
        lanes = pl.ds(pl.multiple_of(h * HEAD, HEAD), HEAD)
        for t in range(rows // TILE):
            span = slice(t * TILE, (t + 1) * TILE)
            scores = dot_nt(q_ref[span, lanes], kl[:, 0:HEAD]) * scale_two + bias_ref[t:t + 1, :]
            top = jnp.max(scores, axis=1, keepdims=True)
            weights = jnp.exp2(scores - top)
            inverse = 1.0 / jnp.sum(weights, axis=1, keepdims=True)
            probs = weights * inverse
            prob_grad = dot_nt(g_ref[0, span, lanes], vl[:, 0:HEAD])
            centre = jnp.sum(probs * prob_grad, axis=1, keepdims=True)
            probs_s[span, :] = probs.astype(jnp.bfloat16)
            grad_s[span, :] = (probs * (prob_grad - centre) * scale_root).astype(jnp.bfloat16)

        q_all = q_ref[:, lanes]
        g_all = g_ref[0, :, lanes]
        q_up = dot_nt(up_ref[1, :, lanes], q_all).astype(jnp.bfloat16)
        g_up = dot_nt(up_ref[2, :, lanes], g_all).astype(jnp.bfloat16)
        rkv[0:rank, :] += dot_nn(q_up, grad_s[...])
        rkv[rank:2 * rank, :] += dot_nn(g_up, probs_s[...])
        att = dot_nn(probs_s[...], vl[...])
        att_ref[0, :, lanes] = att[:, 0:HEAD].astype(jnp.bfloat16)
        low_v = att[:, HEAD:].astype(jnp.bfloat16)
        dq = dot_nn(grad_s[...], kl[...])
        dq_low = dq[:, 0:HEAD].astype(jnp.bfloat16)
        low_k = dq[:, HEAD:].astype(jnp.bfloat16)
        rq_ref[...] += dot_nt(up_ref[0, :, lanes], dq_low)
        gup_ref[0:rank, lanes] = dot_tn(low_ref[...], dq_low)[0:rank, :]
        gup_ref[rank:2 * rank, lanes] = dot_tn(low_k, q_all)[rank:2 * rank, :]
        gup_ref[2 * rank:3 * rank, lanes] = dot_tn(low_v, g_all)[2 * rank:3 * rank, :]
        return carry

    lax.fori_loop(0, heads, one_head, 0)
    returns = []
    for s, peer in enumerate((partner, other)):
        r_out[s] = rkv[:, (s + 1) * rows:(s + 2) * rows]
        returns.append(remote(r_out.at[s], r_in.at[s], r_send.at[s], r_recv.at[s], peer))
        returns[-1].start()
    low_first.wait_send()
    low_next.wait_send()
    each(lambda h: swap(h).wait_send())
    each(lambda h: relay(h).wait_send())
    for copy in returns:
        copy.wait()
    own_ref[...] = rkv[:, 0:rows] + r_in[0] + r_in[1]


def attend(count, bias, q, g, kv, low, up):
    rows, across = q.shape
    heads = across // HEAD
    rank = up.shape[1]
    dma = pltpu.SemaphoreType.DMA
    vmem = pl.BlockSpec(memory_space=pltpu.VMEM)
    bf16, f32 = jnp.bfloat16, jnp.float32
    return pl.pallas_call(
        functools.partial(attend_kernel, rank, count),
        out_shape=[
            jax.ShapeDtypeStruct((1, rows, across), bf16),
            jax.ShapeDtypeStruct((rank, rows), f32),
            jax.ShapeDtypeStruct((2 * rank, rows), f32),
            jax.ShapeDtypeStruct((3 * rank, across), f32),
        ],
        in_specs=[vmem] * 6,
        out_specs=[vmem] * 4,
        scratch_shapes=[
            pltpu.VMEM(kv.shape, bf16), pltpu.VMEM(kv.shape, bf16),
            pltpu.VMEM(low.shape, bf16), pltpu.VMEM(low.shape, bf16),
            pltpu.VMEM((3 * rows, 2 * HEAD), bf16),
            pltpu.VMEM((3 * rows, 2 * HEAD), bf16),
            pltpu.VMEM((rows, 3 * rows), bf16),
            pltpu.VMEM((rows, 3 * rows), bf16),
            pltpu.VMEM((2 * rank, 3 * rows), f32),
            pltpu.VMEM((2, 2 * rank, rows), f32),
            pltpu.VMEM((2, 2 * rank, rows), f32),
            dma((heads,)), dma((heads,)), dma((heads,)), dma((heads,)),
            dma((2,)), dma((2,)), dma((2,)), dma((2,)),
        ],
        compiler_params=pltpu.CompilerParams(
            collective_id=1, has_side_effects=True, vmem_limit_bytes=56 << 20
        ),
        name="attend",
    )(bias, q, g, kv, low, up)


def reduce_kernel(nb, nt, terms_ref, out_ref, first, partial, second, final,
                  send1, recv1, send2, recv2, send3, recv3, send4, recv4):
    mine_b = lax.axis_index("batch")
    mine_t = lax.axis_index("tiles")
    barrier = pltpu.get_barrier_semaphore()
    for d in range(1, nb):
        pl.semaphore_signal(barrier, inc=1, device_id={"batch": lax.rem(mine_b + d, nb)},
                            device_id_type=pl.DeviceIdType.MESH)
    for d in range(1, nt):
        pl.semaphore_signal(barrier, inc=1, device_id={"tiles": lax.rem(mine_t + d, nt)},
                            device_id_type=pl.DeviceIdType.MESH)
    pl.semaphore_wait(barrier, nb + nt - 2)

    def launch(source, target, send, recv, axis, peer):
        copy = pltpu.make_async_remote_copy(
            src_ref=source, dst_ref=target, send_sem=send, recv_sem=recv,
            device_id={axis: peer}, device_id_type=pl.DeviceIdType.MESH,
        )
        copy.start()
        return copy

    copies = []
    for d in range(1, nb):
        peer = lax.rem(mine_b + d, nb)
        copies.append(launch(terms_ref.at[peer], first.at[d - 1], send1.at[d - 1],
                             recv1.at[d - 1], "batch", peer))
    for copy in copies:
        copy.wait()
    total = terms_ref[mine_b].astype(jnp.float32)
    for d in range(nb - 1):
        total = total + first[d].astype(jnp.float32)
    partial[...] = total.astype(jnp.bfloat16)

    copies = []
    for d in range(1, nt):
        peer = lax.rem(mine_t + d, nt)
        copies.append(launch(partial.at[peer], second.at[d - 1], send2.at[d - 1],
                             recv2.at[d - 1], "tiles", peer))
    for copy in copies:
        copy.wait()
    total = partial[mine_t].astype(jnp.float32)
    for d in range(nt - 1):
        total = total + second[d].astype(jnp.float32)
    final[...] = total.astype(jnp.bfloat16)

    copies = []
    for d in range(1, nt):
        peer = lax.rem(mine_t + d, nt)
        copies.append(launch(final, out_ref.at[mine_b, mine_t], send3.at[d - 1],
                             recv3.at[d - 1], "tiles", peer))
    out_ref[mine_b, mine_t] = final[...]
    for copy in copies:
        copy.wait()

    copies = []
    for d in range(1, nb):
        peer = lax.rem(mine_b + d, nb)
        copies.append(launch(out_ref.at[mine_b], out_ref.at[mine_b], send4.at[d - 1],
                             recv4.at[d - 1], "batch", peer))
    for copy in copies:
        copy.wait()


def reduce_all(terms):
    nb, nt, rows, lanes = terms.shape
    dma = pltpu.SemaphoreType.DMA
    return pl.pallas_call(
        functools.partial(reduce_kernel, nb, nt),
        out_shape=jax.ShapeDtypeStruct(terms.shape, jnp.bfloat16),
        in_specs=[pl.BlockSpec(memory_space=pltpu.VMEM)],
        out_specs=pl.BlockSpec(memory_space=pltpu.VMEM),
        scratch_shapes=[
            pltpu.VMEM((nb - 1, nt, rows, lanes), jnp.bfloat16),
            pltpu.VMEM((nt, rows, lanes), jnp.bfloat16),
            pltpu.VMEM((nt - 1, rows, lanes), jnp.bfloat16),
            pltpu.VMEM((rows, lanes), jnp.bfloat16),
            dma((nb - 1,)), dma((nb - 1,)), dma((nt - 1,)), dma((nt - 1,)),
            dma((nt - 1,)), dma((nt - 1,)), dma((nb - 1,)), dma((nb - 1,)),
        ],
        compiler_params=pltpu.CompilerParams(collective_id=0, has_side_effects=True),
        name="reduce_all",
    )(terms)


def summed_everywhere(terms):
    nb, nt = lax.axis_size("batch"), lax.axis_size("tiles")
    rows, columns = terms.shape
    pieces = (rows // 16) * (columns // LANES)
    share = -(-pieces // (nb * nt))
    tiled = terms.astype(jnp.bfloat16).reshape(rows // 16, 16, columns // LANES, LANES)
    tiled = tiled.transpose(0, 2, 1, 3).reshape(pieces, 16, LANES)
    tiled = jnp.pad(tiled, ((0, share * nb * nt - pieces), (0, 0), (0, 0)))
    total = reduce_all(tiled.reshape(nb, nt, share * 16, LANES))
    total = total.reshape(share * nb * nt, 16, LANES)[0:pieces]
    total = total.reshape(rows // 16, columns // LANES, 16, LANES).transpose(0, 2, 1, 3)
    return total.reshape(rows, columns).astype(jnp.float32)


def mask_bias(window_rows, sides, present):
    per_slab = GF * GR
    query_tile = jnp.arange(per_slab, dtype=jnp.int32)
    key_local = jnp.tile(query_tile, 3)
    key_side = jnp.repeat(jnp.stack(sides), per_slab)
    here = jnp.repeat(jnp.stack(present), per_slab)
    frame_step = key_local[None, :] // GR - query_tile[:, None] // GR
    row_step = key_local[None, :] % GR - query_tile[:, None] % GR
    code = (key_side[None, :] * 3 + frame_step + 1) * 3 + row_step + 1
    nearby = (jnp.abs(frame_step) <= 1) & (jnp.abs(row_step) <= 1)
    offsets = jnp.arange(27, dtype=jnp.int32)
    listed = jnp.sum(
        jnp.where(code[:, :, None] == offsets[None, None, :], window_rows[:, None, :], 0), axis=2
    )
    allowed = nearby & here[None, :] & (listed > 0)
    return jnp.repeat(jnp.where(allowed, 0.0, -1e30).astype(jnp.float32), TILE, axis=1)


def per_device(
    hidden,
    frozen_queries,
    frozen_keys,
    frozen_values,
    reward_output_gradient,
    truncation_step,
    modulation,
    adapter_down_weight,
    adapter_up_weight,
    window,
):
    slab_rows, width = hidden.shape[1:]
    across = frozen_queries.shape[2]
    rank = adapter_up_weight.shape[1]
    count = lax.axis_size("tiles")
    index = lax.axis_index("tiles")
    even = index % 2 == 0
    down_cat = jnp.concatenate(
        [adapter_down_weight[j] for j in range(3)]
        + [jnp.zeros((width, LANES - 3 * rank), jnp.bfloat16)], axis=1
    )
    up_pad = jnp.stack([
        jnp.pad(adapter_up_weight[j], ((j * rank, LANES - (j + 1) * rank), (0, 0)))
        for j in range(3)
    ])
    x_low, low, queries, kv = project(
        truncation_step, hidden, modulation, down_cat, up_pad,
        frozen_queries, frozen_keys, frozen_values,
    )

    zero, one, two = (jnp.int32(i) for i in range(3))
    swap_side = jnp.where(even, two, zero)
    relay_side = jnp.where(even, zero, two)
    relay_here = jnp.where(even, index >= 1, index < count - 1)
    bias = mask_bias(
        window, (one, swap_side, relay_side), (jnp.bool_(True), jnp.bool_(True), relay_here)
    )

    attended, rq_total, owned, ups = attend(
        count, bias, queries, reward_output_gradient, kv, low, adapter_up_weight
    )
    rank_grads = jnp.concatenate([rq_total, owned], axis=0).astype(jnp.bfloat16)
    down_terms = jnp.dot(rank_grads, x_low, preferred_element_type=jnp.float32)
    norm_factor = 1.0 / math.sqrt(
        hidden.shape[0] * lax.axis_size("batch") * slab_rows * count
    )
    terms = jnp.concatenate([down_terms, ups], axis=1) * norm_factor
    total = summed_everywhere(terms)
    grad_down = total[:, 0:width].reshape(3, rank, width).transpose(0, 2, 1)
    grad_up = total[:, width:].reshape(3, rank, across)
    return (attended, grad_down, grad_up)


def solution(mesh):
    placed = (
        P("batch", "tiles", None),
        P("batch", "tiles", None),
        P("batch", "tiles", None),
        P("batch", "tiles", None),
        P("batch", "tiles", None),
        P("batch"),
        P(),
        P(),
        P(),
        P("tiles", None),
    )
    return jax.shard_map(
        per_device,
        mesh=mesh,
        in_specs=placed,
        out_specs=(P("batch", "tiles", None), P(), P()),
        check_vma=False,
    )
```

```python
import functools
import math

import jax
import jax.numpy as jnp
from jax import lax
from jax.experimental import pallas as pl
from jax.experimental.pallas import tpu as pltpu
from jax.sharding import PartitionSpec as P

HEAD = 128
TILE = 128
GF = 2
GR = 2
LANES = 128


def dot_nt(a, b):
    return lax.dot_general(
        a, b, (((1,), (1,)), ((), ())), preferred_element_type=jnp.float32
    )


def dot_tn(a, b):
    return lax.dot_general(
        a, b, (((0,), (0,)), ((), ())), preferred_element_type=jnp.float32
    )


def dot_nn(a, b):
    return jnp.dot(a, b, preferred_element_type=jnp.float32)


def project_kernel(step_ref, hidden_ref, mod_ref, down_ref, up_ref, fq_ref, fk_ref, fv_ref,
                   x_ref, low_ref, q_ref, kv_ref):
    x = hidden_ref[0].astype(jnp.float32)
    width = x.shape[1]
    mean = jnp.sum(x, axis=1, keepdims=True) * (1.0 / width)
    centred = x - mean
    variance = jnp.sum(centred * centred, axis=1, keepdims=True) * (1.0 / width)
    normed = centred * lax.rsqrt(variance + 1e-06)
    modulated = normed * (1.0 + mod_ref[0, 1:2, :]) + mod_ref[0, 0:1, :]
    x_low = modulated.astype(jnp.bfloat16)
    x_ref[...] = x_low
    rank = up_ref.shape[1]
    low_ref[...] = jnp.zeros_like(low_ref)
    sums = []
    for j, frozen_ref in enumerate((fq_ref, fk_ref, fv_ref)):
        low = dot_nt(x_low, down_ref[j]).astype(jnp.bfloat16)
        low_ref[:, j * rank:(j + 1) * rank] = low
        total = frozen_ref[0].astype(jnp.float32) + dot_nn(low, up_ref[j])
        sums.append(total.astype(jnp.bfloat16))
    q_ref[...], keys, values = sums
    for h in range(keys.shape[1] // HEAD):
        kv_ref[h, :, 0:HEAD] = keys[:, h * HEAD:(h + 1) * HEAD]
        kv_ref[h, :, HEAD:] = values[:, h * HEAD:(h + 1) * HEAD]


def project(step, hidden, modulation, down, up, fq, fk, fv):
    _, rows, width = hidden.shape
    across = fq.shape[2]
    block = TILE
    heads = across // HEAD
    row3 = lambda i, s: (0, i, 0)
    row2 = lambda i, s: (i, 0)
    return pl.pallas_call(
        project_kernel,
        out_shape=[
            jax.ShapeDtypeStruct((rows, width), jnp.bfloat16),
            jax.ShapeDtypeStruct((rows, LANES), jnp.bfloat16),
            jax.ShapeDtypeStruct((rows, across), jnp.bfloat16),
            jax.ShapeDtypeStruct((heads, rows, 2 * HEAD), jnp.bfloat16),
        ],
        grid_spec=pltpu.PrefetchScalarGridSpec(
            num_scalar_prefetch=1,
            grid=(rows // block,),
            in_specs=[
                pl.BlockSpec((1, block, width), row3),
                pl.BlockSpec((1, 2, width), lambda i, s: (s[0], 0, 0)),
                pl.BlockSpec(down.shape, lambda i, s: (0, 0, 0)),
                pl.BlockSpec(up.shape, lambda i, s: (0, 0, 0)),
                pl.BlockSpec((1, block, across), row3),
                pl.BlockSpec((1, block, across), row3),
                pl.BlockSpec((1, block, across), row3),
            ],
            out_specs=[
                pl.BlockSpec((block, width), row2),
                pl.BlockSpec((block, LANES), row2),
                pl.BlockSpec((block, across), row2),
                pl.BlockSpec((heads, block, 2 * HEAD), lambda i, s: (0, i, 0)),
            ],
        ),
        name="project",
    )(step, hidden, modulation, down, up, fq, fk, fv)


def attend_kernel(rank, count, bias_ref, low_ref, up_ref, q_hbm, g_hbm, kv_hbm,
                  att_ref, rq_ref, own_ref, gup_ref,
                  q_ref, g_ref, kv_ref, kv_swap, kv_relay, low_swap, low_relay, kl, vl, probs_s, grad_s, rkv,
                  r_out, r_in, swap_send, swap_recv, relay_send, relay_recv,
                  low_send, low_recv, r_send, r_recv, load):
    heads, rows = kv_ref.shape[0], q_ref.shape[0]
    index = lax.axis_index("tiles")
    odd = lax.rem(index, 2)
    partner = index + 1 - 2 * odd
    target = lax.rem(index + 2 - 4 * odd + count, count)
    source = lax.rem(index - 2 + 4 * odd + count, count)
    other = lax.rem(index - 1 + 2 * odd + count, count)
    barrier = pltpu.get_barrier_semaphore()
    for peer in (partner, target, source, other):
        pl.semaphore_signal(barrier, inc=1, device_id={"tiles": peer},
                            device_id_type=pl.DeviceIdType.MESH)
    pl.semaphore_wait(barrier, 4)

    def remote(src, dst, send, recv, peer):
        return pltpu.make_async_remote_copy(
            src_ref=src, dst_ref=dst, send_sem=send, recv_sem=recv,
            device_id={"tiles": peer}, device_id_type=pl.DeviceIdType.MESH,
        )

    def swap(h):
        return remote(kv_hbm.at[h], kv_swap.at[h], swap_send.at[h], swap_recv.at[h], partner)

    def relay(h):
        return remote(kv_swap.at[h], kv_relay.at[h], relay_send.at[h], relay_recv.at[h], target)

    def each(step):
        lax.fori_loop(0, heads, lambda h, c: (step(h), c)[1], 0)

    low_first = remote(low_ref, low_swap, low_send.at[0], low_recv.at[0], partner)
    low_next = remote(low_swap, low_relay, low_send.at[1], low_recv.at[1], target)
    low_first.start()
    each(lambda h: swap(h).start())
    loads = [
        pltpu.make_async_copy(src, dst, load.at[i])
        for i, (src, dst) in enumerate(((q_hbm, q_ref), (g_hbm, g_ref), (kv_hbm, kv_ref)))
    ]
    for copy in loads:
        copy.start()
    rq_ref[...] = jnp.zeros_like(rq_ref)
    rkv[...] = jnp.zeros_like(rkv)
    for copy in loads:
        copy.wait()
    low_first.wait_recv()
    low_next.start()
    swap(0).wait_recv()
    relay(0).start()
    low_next.wait_recv()
    for s, low in enumerate((low_ref, low_swap, low_relay)):
        kl[s * rows:(s + 1) * rows, HEAD:] = low[...]
        vl[s * rows:(s + 1) * rows, HEAD:] = low[...]
    scale_root = 1.0 / math.sqrt(HEAD)
    scale_two = scale_root * math.log2(math.e)

    def one_head(h, carry):
        @pl.when(h + 1 < heads)
        def _():
            swap(h + 1).wait_recv()
            relay(h + 1).start()

        relay(h).wait_recv()
        for s, part in enumerate((kv_ref, kv_swap, kv_relay)):
            kl[s * rows:(s + 1) * rows, 0:HEAD] = part[h, :, 0:HEAD]
            vl[s * rows:(s + 1) * rows, 0:HEAD] = part[h, :, HEAD:]
        lanes = pl.ds(pl.multiple_of(h * HEAD, HEAD), HEAD)
        for t in range(rows // TILE):
            span = slice(t * TILE, (t + 1) * TILE)
            scores = dot_nt(q_ref[span, lanes], kl[:, 0:HEAD]) * scale_two + bias_ref[t:t + 1, :]
            top = jnp.max(scores, axis=1, keepdims=True)
            weights = jnp.exp2(scores - top)
            inverse = 1.0 / jnp.sum(weights, axis=1, keepdims=True)
            probs = weights * inverse
            prob_grad = dot_nt(g_ref[0, span, lanes], vl[:, 0:HEAD])
            centre = jnp.sum(probs * prob_grad, axis=1, keepdims=True)
            probs_s[span, :] = probs.astype(jnp.bfloat16)
            grad_s[span, :] = (probs * (prob_grad - centre) * scale_root).astype(jnp.bfloat16)

        q_all = q_ref[:, lanes]
        g_all = g_ref[0, :, lanes]
        q_up = dot_nt(up_ref[1, :, lanes], q_all).astype(jnp.bfloat16)
        g_up = dot_nt(up_ref[2, :, lanes], g_all).astype(jnp.bfloat16)
        rkv[0:rank, :] += dot_nn(q_up, grad_s[...])
        rkv[rank:2 * rank, :] += dot_nn(g_up, probs_s[...])
        att = dot_nn(probs_s[...], vl[...])
        att_ref[0, :, lanes] = att[:, 0:HEAD].astype(jnp.bfloat16)
        low_v = att[:, HEAD:].astype(jnp.bfloat16)
        dq = dot_nn(grad_s[...], kl[...])
        dq_low = dq[:, 0:HEAD].astype(jnp.bfloat16)
        low_k = dq[:, HEAD:].astype(jnp.bfloat16)
        rq_ref[...] += dot_nt(up_ref[0, :, lanes], dq_low)
        gup_ref[0:rank, lanes] = dot_tn(low_ref[...], dq_low)[0:rank, :]
        gup_ref[rank:2 * rank, lanes] = dot_tn(low_k, q_all)[rank:2 * rank, :]
        gup_ref[2 * rank:3 * rank, lanes] = dot_tn(low_v, g_all)[2 * rank:3 * rank, :]
        return carry

    lax.fori_loop(0, heads, one_head, 0)
    returns = []
    for s, peer in enumerate((partner, other)):
        r_out[s] = rkv[:, (s + 1) * rows:(s + 2) * rows]
        returns.append(remote(r_out.at[s], r_in.at[s], r_send.at[s], r_recv.at[s], peer))
        returns[-1].start()
    low_first.wait_send()
    low_next.wait_send()
    each(lambda h: swap(h).wait_send())
    each(lambda h: relay(h).wait_send())
    for copy in returns:
        copy.wait()
    own_ref[...] = rkv[:, 0:rows] + r_in[0] + r_in[1]


def attend(count, bias, q, g, kv, low, up):
    rows, across = q.shape
    heads = across // HEAD
    rank = up.shape[1]
    dma = pltpu.SemaphoreType.DMA
    vmem = pl.BlockSpec(memory_space=pltpu.VMEM)
    bf16, f32 = jnp.bfloat16, jnp.float32
    return pl.pallas_call(
        functools.partial(attend_kernel, rank, count),
        out_shape=[
            jax.ShapeDtypeStruct((1, rows, across), bf16),
            jax.ShapeDtypeStruct((rank, rows), f32),
            jax.ShapeDtypeStruct((2 * rank, rows), f32),
            jax.ShapeDtypeStruct((3 * rank, across), f32),
        ],
        in_specs=[vmem] * 3 + [pl.BlockSpec(memory_space=pl.ANY)] * 3,
        out_specs=[vmem] * 4,
        scratch_shapes=[
            pltpu.VMEM(q.shape, bf16), pltpu.VMEM(g.shape, bf16),
            pltpu.VMEM(kv.shape, bf16), pltpu.VMEM(kv.shape, bf16), pltpu.VMEM(kv.shape, bf16),
            pltpu.VMEM(low.shape, bf16), pltpu.VMEM(low.shape, bf16),
            pltpu.VMEM((3 * rows, 2 * HEAD), bf16),
            pltpu.VMEM((3 * rows, 2 * HEAD), bf16),
            pltpu.VMEM((rows, 3 * rows), bf16),
            pltpu.VMEM((rows, 3 * rows), bf16),
            pltpu.VMEM((2 * rank, 3 * rows), f32),
            pltpu.VMEM((2, 2 * rank, rows), f32),
            pltpu.VMEM((2, 2 * rank, rows), f32),
            dma((heads,)), dma((heads,)), dma((heads,)), dma((heads,)),
            dma((2,)), dma((2,)), dma((2,)), dma((2,)), dma((3,)),
        ],
        compiler_params=pltpu.CompilerParams(
            collective_id=1, has_side_effects=True, vmem_limit_bytes=56 << 20
        ),
        name="attend",
    )(bias, low, up, q, g, kv)


def reduce_kernel(nb, nt, terms_ref, out_ref, first, partial, second, final,
                  send1, recv1, send2, recv2, send3, recv3, send4, recv4):
    mine_b = lax.axis_index("batch")
    mine_t = lax.axis_index("tiles")
    barrier = pltpu.get_barrier_semaphore()
    for d in range(1, nb):
        pl.semaphore_signal(barrier, inc=1, device_id={"batch": lax.rem(mine_b + d, nb)},
                            device_id_type=pl.DeviceIdType.MESH)
    for d in range(1, nt):
        pl.semaphore_signal(barrier, inc=1, device_id={"tiles": lax.rem(mine_t + d, nt)},
                            device_id_type=pl.DeviceIdType.MESH)
    pl.semaphore_wait(barrier, nb + nt - 2)

    def launch(source, target, send, recv, axis, peer):
        copy = pltpu.make_async_remote_copy(
            src_ref=source, dst_ref=target, send_sem=send, recv_sem=recv,
            device_id={axis: peer}, device_id_type=pl.DeviceIdType.MESH,
        )
        copy.start()
        return copy

    peers_b = [lax.rem(mine_b + d, nb) for d in range(1, nb)]
    peers_t = [lax.rem(mine_t + 1 + e, nt) for e in range(nt)]
    sent = []
    scatter = []
    for e in range(nt):
        scatter.append([
            launch(terms_ref.at[peer, peers_t[e]], first.at[d, e], send1.at[d, e],
                   recv1.at[d, e], "batch", peer)
            for d, peer in enumerate(peers_b)
        ])
        sent += scatter[-1]
    across = []
    for e in range(nt):
        total = terms_ref[mine_b, peers_t[e]].astype(jnp.float32)
        for d in range(nb - 1):
            scatter[e][d].wait_recv()
            total = total + first[d, e].astype(jnp.float32)
        if e < nt - 1:
            partial[e] = total.astype(jnp.bfloat16)
            across.append(launch(partial.at[e], second.at[e], send2.at[e], recv2.at[e],
                                 "tiles", peers_t[e]))
    for e in range(nt - 1):
        across[e].wait_recv()
        total = total + second[e].astype(jnp.float32)
    final[...] = total.astype(jnp.bfloat16)

    gather = [
        launch(final, out_ref.at[mine_b, mine_t], send3.at[e], recv3.at[e], "tiles", peers_t[e])
        for e in range(nt - 1)
    ]
    last = [
        launch(final, out_ref.at[mine_b, mine_t], send4.at[d, nt - 1], recv4.at[d, nt - 1],
               "batch", peer)
        for d, peer in enumerate(peers_b)
    ]
    out_ref[mine_b, mine_t] = final[...]
    for e in range(nt - 1):
        gather[e].wait_recv()
        origin = lax.rem(mine_t - 1 - e + nt, nt)
        block = out_ref.at[mine_b, origin]
        last += [
            launch(block, block, send4.at[d, e], recv4.at[d, e], "batch", peer)
            for d, peer in enumerate(peers_b)
        ]
    for copy in last:
        copy.wait_recv()
    for copy in sent + across + gather + last:
        copy.wait_send()


def reduce_all(terms):
    nb, nt, rows, lanes = terms.shape
    dma = pltpu.SemaphoreType.DMA
    return pl.pallas_call(
        functools.partial(reduce_kernel, nb, nt),
        out_shape=jax.ShapeDtypeStruct(terms.shape, jnp.bfloat16),
        in_specs=[pl.BlockSpec(memory_space=pltpu.VMEM)],
        out_specs=pl.BlockSpec(memory_space=pltpu.VMEM),
        scratch_shapes=[
            pltpu.VMEM((nb - 1, nt, rows, lanes), jnp.bfloat16),
            pltpu.VMEM((nt - 1, rows, lanes), jnp.bfloat16),
            pltpu.VMEM((nt - 1, rows, lanes), jnp.bfloat16),
            pltpu.VMEM((rows, lanes), jnp.bfloat16),
            dma((nb - 1, nt)), dma((nb - 1, nt)), dma((nt - 1,)), dma((nt - 1,)),
            dma((nt - 1,)), dma((nt - 1,)), dma((nb - 1, nt)), dma((nb - 1, nt)),
        ],
        compiler_params=pltpu.CompilerParams(collective_id=0, has_side_effects=True),
        name="reduce_all",
    )(terms)


def summed_everywhere(terms):
    nb, nt = lax.axis_size("batch"), lax.axis_size("tiles")
    rows, columns = terms.shape
    pieces = (rows // 16) * (columns // LANES)
    share = -(-pieces // (nb * nt))
    tiled = terms.astype(jnp.bfloat16).reshape(rows // 16, 16, columns // LANES, LANES)
    tiled = tiled.transpose(0, 2, 1, 3).reshape(pieces, 16, LANES)
    tiled = jnp.pad(tiled, ((0, share * nb * nt - pieces), (0, 0), (0, 0)))
    total = reduce_all(tiled.reshape(nb, nt, share * 16, LANES))
    total = total.reshape(share * nb * nt, 16, LANES)[0:pieces]
    total = total.reshape(rows // 16, columns // LANES, 16, LANES).transpose(0, 2, 1, 3)
    return total.reshape(rows, columns).astype(jnp.float32)


def mask_bias(window_rows, sides, present):
    per_slab = GF * GR
    query_tile = jnp.arange(per_slab, dtype=jnp.int32)
    key_local = jnp.tile(query_tile, 3)
    key_side = jnp.repeat(jnp.stack(sides), per_slab)
    here = jnp.repeat(jnp.stack(present), per_slab)
    frame_step = key_local[None, :] // GR - query_tile[:, None] // GR
    row_step = key_local[None, :] % GR - query_tile[:, None] % GR
    code = (key_side[None, :] * 3 + frame_step + 1) * 3 + row_step + 1
    nearby = (jnp.abs(frame_step) <= 1) & (jnp.abs(row_step) <= 1)
    offsets = jnp.arange(27, dtype=jnp.int32)
    listed = jnp.sum(
        jnp.where(code[:, :, None] == offsets[None, None, :], window_rows[:, None, :], 0), axis=2
    )
    allowed = nearby & here[None, :] & (listed > 0)
    return jnp.repeat(jnp.where(allowed, 0.0, -1e30).astype(jnp.float32), TILE, axis=1)


def per_device(
    hidden,
    frozen_queries,
    frozen_keys,
    frozen_values,
    reward_output_gradient,
    truncation_step,
    modulation,
    adapter_down_weight,
    adapter_up_weight,
    window,
):
    slab_rows, width = hidden.shape[1:]
    across = frozen_queries.shape[2]
    rank = adapter_up_weight.shape[1]
    count = lax.axis_size("tiles")
    index = lax.axis_index("tiles")
    even = index % 2 == 0
    down_rows = adapter_down_weight.transpose(0, 2, 1)
    x_low, low, queries, kv = project(
        truncation_step, hidden, modulation, down_rows, adapter_up_weight,
        frozen_queries, frozen_keys, frozen_values,
    )

    zero, one, two = (jnp.int32(i) for i in range(3))
    swap_side = jnp.where(even, two, zero)
    relay_side = jnp.where(even, zero, two)
    relay_here = jnp.where(even, index >= 1, index < count - 1)
    bias = mask_bias(
        window, (one, swap_side, relay_side), (jnp.bool_(True), jnp.bool_(True), relay_here)
    )

    attended, rq_total, owned, ups = attend(
        count, bias, queries, reward_output_gradient, kv, low, adapter_up_weight
    )
    rank_grads = jnp.concatenate([rq_total, owned], axis=0).astype(jnp.bfloat16)
    down_terms = jnp.dot(rank_grads, x_low, preferred_element_type=jnp.float32)
    norm_factor = 1.0 / math.sqrt(
        hidden.shape[0] * lax.axis_size("batch") * slab_rows * count
    )
    terms = jnp.concatenate([down_terms, ups], axis=1) * norm_factor
    total = summed_everywhere(terms)
    grad_down = total[:, 0:width].reshape(3, rank, width).transpose(0, 2, 1)
    grad_up = total[:, width:].reshape(3, rank, across)
    return (attended, grad_down, grad_up)


def solution(mesh):
    placed = (
        P("batch", "tiles", None),
        P("batch", "tiles", None),
        P("batch", "tiles", None),
        P("batch", "tiles", None),
        P("batch", "tiles", None),
        P("batch"),
        P(),
        P(),
        P(),
        P("tiles", None),
    )
    return jax.shard_map(
        per_device,
        mesh=mesh,
        in_specs=placed,
        out_specs=(P("batch", "tiles", None), P(), P()),
        check_vma=False,
    )
```
